32 devices in a mesh: sym: 4 (over y, core), slab: 8 (over z, x).
Axes of the slice: x: 2, y: 2, z: 4, core: 2. Of those that a mesh axis runs over, the one named last changes fastest.
Arguments:
- coefficients: float32 [8, 8192, 128], P('sym', 'slab'), may hold values from -6 to 6
- dipole: bfloat16 [8, 8192, 8192], P('sym', 'slab'), may hold values from -0.09375 to 0.09375
- energies: float32 [8, 8192], P('sym', 'slab'), may hold values from -3 to 3
- pulse_field: float32 [64], replicated, may hold values from 0.5 to 2
- live_states: int32 [8], replicated, may hold values from 4096 to 8192, as said below
Outputs:
- adjoint: float32 [8, 8192, 128], P('sym', 'slab')
The draws below stay inside these ranges and needn't reach their ends.
Inputs may be any that keep to these rules, and one draw needn't show every extreme that they name: live_states[L] counts the states in use in symmetry block L; positions at or beyond it are padding; some block uses all 8192.
All inputs are finite; a program needn't handle non-finite values.
Results may differ from the reference program's by a relative error of at most 0.0012.
Values may be sent and summed in bfloat16 or wider, within the bound.
A program may use at most 128 MiB of HBM per device.

```python
import math
import jax
import jax.numpy as jnp
from jax import lax

K = 8192
C = 64
NSYM = 8


def draw_live_states(key, part):
    counts = jax.random.randint(key, (NSYM,), K // 2, K + 1)
    full_block = jax.random.randint(jax.random.fold_in(key, 11), (), 0, NSYM)
    return counts.at[full_block].set(K).astype(jnp.int32)


def spiked(entries, key, source, target, blocks, factor):
    def block_of(axis_at):
        return (jnp.arange(entries.shape[axis_at]) // (entries.shape[axis_at] // blocks)).reshape((-1,) + (1,) * (entries.ndim - 1 - axis_at))

    one_side = jax.random.permutation(key, blocks)[block_of(target)]
    second = (block_of(target) + blocks // 2) % blocks
    return jnp.where((block_of(source) == one_side) | (block_of(source) == second), factor * entries, entries)


def steps_of(key, dims, shards, least, high):
    def one(position, parts):
        steps = jax.random.uniform(jax.random.fold_in(jax.random.fold_in(key, 6), position), (parts,), jnp.float32, least / len(shards), high / len(shards))
        return jnp.repeat(jnp.exp(steps), dims[position] // parts).reshape((-1,) + (1,) * (len(dims) - position - 1))

    gain = one(*shards[0])
    for cut in shards[1:]:
        gain = gain * one(*cut)
    return gain


def normal_values(stream_key, extent, scale, limit, shards=(), kind=jnp.bfloat16):
    result = scale * jax.random.normal(stream_key, extent, jnp.float32)
    if shards:
        result = result * steps_of(stream_key, extent, shards, -0.22, 0.18)
    return jnp.clip(result, -limit, limit).astype(kind)


def heavy_noise(own_key, extent, deviation, bound, shards, heavy, held_as=jnp.bfloat16):
    result = deviation * jax.random.normal(own_key, extent, jnp.float32)
    if shards:
        result = result * steps_of(own_key, extent, shards, -0.22, 0.18)
    return jnp.clip(spiked(result, jax.random.fold_in(own_key, 3), *heavy), -bound, bound).astype(held_as)


def setup_inputs(seed: int = 0) -> dict:
    arg_keys = jax.random.split(jax.random.key(seed), 6)
    return {
        "coefficients": normal_values(arg_keys[0], (NSYM, K, 2 * C), 1.0, 6.0, ((0, 4), (1, 8)), jnp.float32),
        "dipole": heavy_noise(arg_keys[1], (NSYM, K, K), K ** -0.5, 0.09375, ((0, 4), (1, 8)), (1, 2, 8, 2.0)),
        "energies": jnp.clip(jax.random.uniform(arg_keys[2], (NSYM, K), jnp.float32, -3.0, 3.0) * steps_of(arg_keys[2], (NSYM, K), ((0, 4), (1, 8)), -0.4, 0.0), -3.0, 3.0),
        "pulse_field": jnp.clip(jnp.exp(jax.random.uniform(arg_keys[3], (C,), jnp.float32, math.log(0.5), math.log(2.0))), 0.5, 2.0),
        "live_states": draw_live_states(jax.random.fold_in(arg_keys[5], 71), 0),
    }


step_size = 0.2


def rotate(values):
    half = values.shape[-1] // 2
    return jnp.concatenate([-values[..., half:], values[..., :half]], axis=-1)


def hamiltonian(amplitude, dipole, energies, column_gain, live_mask, upper_on):
    amplitude_bf = amplitude.astype(jnp.bfloat16)
    shifted = jnp.concatenate([amplitude_bf[1:], jnp.zeros_like(amplitude_bf[:1])], axis=0)

    def block_products(items):
        dip_block, upper_rows, own_rows = items
        forward = jnp.dot(dip_block, upper_rows, preferred_element_type=jnp.float32)
        backward = lax.dot_general(dip_block, own_rows, (((0,), (0,)), ((), ())), preferred_element_type=jnp.float32)
        return forward, backward

    forward, backward = lax.map(block_products, (dipole, shifted, amplitude_bf))
    forward = forward * upper_on[:, None, None]
    backward = backward * upper_on[:, None, None]
    lowered = jnp.concatenate([jnp.zeros_like(backward[:1]), backward[:-1]], axis=0)
    return live_mask[:, :, None] * (energies[:, :, None] * amplitude + column_gain * (forward + lowered))


def reference(coefficients, dipole, energies, pulse_field, live_states):
    positions = jnp.arange(K, dtype=jnp.int32)
    live_mask = (positions[None, :] < live_states[:, None]).astype(jnp.float32)
    block_ids = jnp.arange(NSYM, dtype=jnp.int32)
    upper_on = (block_ids < NSYM - 1).astype(jnp.float32)
    column_gain = jnp.concatenate([pulse_field, pulse_field])
    start_state = live_mask[:, :, None] * coefficients
    first_term = step_size * rotate(hamiltonian(start_state, dipole, energies, column_gain, live_mask, upper_on))
    second_term = (0.5 * step_size) * rotate(hamiltonian(first_term, dipole, energies, column_gain, live_mask, upper_on))
    return start_state + first_term + second_term
```

```python
import functools

import jax
import jax.numpy as jnp
from jax import lax
from jax.experimental import pallas as pl
from jax.experimental.pallas import tpu as pltpu
from jax.sharding import PartitionSpec as P

step_size = 0.2
MESH = pl.DeviceIdType.MESH


def kernel(
    n, n_sym_dev, start_ref, dip_ref, energy_ref, mask_ref, gain_ref, out_ref,
    dip, gath, rs_send, rs_recv, u_rows, u_cols, acc, state, low, low_send, low_recv,
    load_sem, start_sem, ag_send_sem, ag_recv_sem, rs_send_sem, rs_recv_sem, sym_send_sem, sym_recv_sem,
):
    n_local, cols, rows = out_ref.shape
    width = dip.shape[-1]
    half = n // 2
    last = n_local - 1
    side = rows // 2
    mid = cols // 2
    s = lax.axis_index("sym")
    me = lax.axis_index("slab")
    odd = me % 2
    pos = (1 - odd) * (me // 2) + odd * (n - 1 - me // 2)

    def at(offset):
        place = (pos + offset + n) % n
        back = place // half
        return (1 - back) * (2 * place) + back * (2 * (n - place) - 1)

    ring = (at(1), at(-1))
    sym_up = (s + 1) % n_sym_dev
    sym_down = (s + n_sym_dev - 1) % n_sym_dev
    sign = (1, -1)

    barrier = pltpu.get_barrier_semaphore()
    for peer in ((s, ring[0]), (s, ring[1]), (sym_up, me), (sym_down, me)):
        pl.semaphore_signal(barrier, inc=1, device_id=peer, device_id_type=MESH)

    def load(b, d):
        j = at(half + d)
        return pltpu.make_async_copy(
            dip_ref.at[b, :, pl.ds(pl.multiple_of(j * width, width), width)],
            dip.at[b, j],
            load_sem.at[b, d],
        )

    first_state = pltpu.make_async_copy(start_ref, state, start_sem)
    first_state.start()
    for b in reversed(range(n_local)):
        load(b, 0).start()

    def start_rest(d, carry):
        for b in range(n_local):
            load(b, d).start()
        return carry

    def wait_rest(d, carry):
        for b in range(n_local):
            load(b, d).wait()
        return carry

    lax.fori_loop(1, n, start_rest, 0)
    first_state.wait()
    out_ref[...] = state[...]
    pl.semaphore_wait(barrier, 4)

    def step(h, carry):
        def ag_copy(b, g, k, owner):
            slot = gath.at[h, b, owner]
            if k == half - 1:
                slot = gath.at[h, b, owner, pl.ds(g * side, side)]
            return pltpu.make_async_remote_copy(
                src_ref=slot, dst_ref=slot,
                send_sem=ag_send_sem.at[h, b, g, k], recv_sem=ag_recv_sem.at[h, b, g, k],
                device_id=(s, ring[g]), device_id_type=MESH,
            )

        def ag_out(b, g, k):
            return ag_copy(b, g, k, at(-sign[g] * k))

        def ag_in(b, g, k):
            return ag_copy(b, g, k, at(-sign[g] * (k + 1)))

        def rs_copy(b, g, k):
            source, target = rs_send.at[b, g, k], rs_recv.at[h, b, g, k]
            if k == 0:
                piece = pl.ds(g * mid, mid)
                source, target = rs_send.at[b, g, k, piece], rs_recv.at[h, b, g, k, piece]
            return pltpu.make_async_remote_copy(
                src_ref=source, dst_ref=target,
                send_sem=rs_send_sem.at[h, b, g, k], recv_sem=rs_recv_sem.at[h, b, g, k],
                device_id=(s, ring[g]), device_id_type=MESH,
            )

        def sym_rows():
            return pltpu.make_async_remote_copy(
                src_ref=u_rows, dst_ref=gath.at[h, last, me],
                send_sem=sym_send_sem.at[h, 0], recv_sem=sym_recv_sem.at[h, 0],
                device_id=(sym_down, me), device_id_type=MESH,
            )

        def sym_low():
            return pltpu.make_async_remote_copy(
                src_ref=low_send, dst_ref=low_recv.at[h],
                send_sem=sym_send_sem.at[h, 1], recv_sem=sym_recv_sem.at[h, 1],
                device_id=(sym_up, me), device_id_type=MESH,
            )

        tile = min(256, width)

        def over_tiles(b, j, emit):
            def one(t, c):
                piece = pl.ds(pl.multiple_of(t * tile, tile), tile)
                emit(piece, jnp.dot(u_cols[b], dip[b, j, :, piece], preferred_element_type=jnp.float32))
                return c

            lax.fori_loop(0, width // tile, one, 0)

        def rs_first(b):
            def emit(piece, value):
                value = value.astype(jnp.bfloat16)
                rs_send[b, 0, 0, :mid, piece] = value[:mid]
                rs_send[b, 1, 0, mid:, piece] = value[mid:]

            over_tiles(b, at(half), emit)
            for g in range(2):
                rs_copy(b, g, 0).start()

        def add_hop(b, g, k, piece, value):
            if k == 0:
                got = rs_recv[h, b, g, 0, g * mid:(g + 1) * mid, piece].astype(jnp.float32)
                parts = [value[:mid], value[mid:]]
                parts[g] = parts[g] + got
                return jnp.concatenate(parts, axis=0)
            return value + rs_recv[h, b, g, k, :, piece].astype(jnp.float32)

        def rs_hop(b, g, k):
            rs_copy(b, g, k - 1).wait_recv()

            def emit(piece, value):
                rs_send[b, g, k, :, piece] = add_hop(b, g, k - 1, piece, value).astype(jnp.bfloat16)

            over_tiles(b, at(sign[g] * (half - k)), emit)
            rs_copy(b, g, k).start()

        def rs_last(b, target):
            for g in range(2):
                rs_copy(b, g, half - 1).wait_recv()

            def emit(piece, value):
                for g in range(2):
                    value = add_hop(b, g, half - 1, piece, value)
                target[:, piece] = value

            over_tiles(b, me, emit)

        row_tile = min(256, rows)

        def forward(b, j, first=False):
            def one(t, c):
                piece = pl.ds(pl.multiple_of(t * row_tile, row_tile), row_tile)
                value = jnp.dot(dip[b, j, piece, :], gath[h, b, j], preferred_element_type=jnp.float32)
                acc[b, piece, :] = value if first else acc[b, piece, :] + value
                return c

            lax.fori_loop(0, rows // row_tile, one, 0)

        u_rows[...] = state[0].T.astype(jnp.bfloat16)
        sym_rows().start()
        for b in range(last):
            gath[h, b, me] = state[b + 1].T.astype(jnp.bfloat16)
            for g in range(2):
                ag_out(b, g, 0).start()
        for b in range(n_local):
            u_cols[b] = state[b].astype(jnp.bfloat16)

        for b in reversed(range(n_local)):
            @pl.when(h == 0)
            def _():
                load(b, 0).wait()

            rs_first(b)
            if b == last:
                sym_rows().wait_recv()
                for g in range(2):
                    ag_out(last, g, 0).start()

        @pl.when(h == 0)
        def _():
            lax.fori_loop(1, n, wait_rest, 0)

        for b in range(n_local):
            forward(b, me, first=True)

        for k in range(1, half):
            for b in range(n_local):
                for g in range(2):
                    ag_in(b, g, k - 1).wait_recv()
                    ag_out(b, g, k).start()
                for g in range(2):
                    rs_hop(last - b, g, k)
            for b in range(n_local):
                for g in range(2):
                    forward(b, at(-sign[g] * k))

        rs_last(last, low_send)
        sym_low().start()
        for b in range(last):
            rs_last(b, low.at[b])
        for b in range(n_local):
            for g in range(2):
                ag_in(b, g, half - 1).wait_recv()
            forward(b, at(half))

        sym_low().wait_recv()
        scale = step_size / (h + 1).astype(jnp.float32)
        for b in range(n_local):
            upper = acc[b].T
            if b == 0:
                lower = low_recv[h] * (s > 0).astype(jnp.float32)
            else:
                lower = low[b - 1]
            if b == last:
                upper = upper * (s < n_sym_dev - 1).astype(jnp.float32)
            applied = mask_ref[b] * (energy_ref[b] * state[b] + gain_ref[...] * (upper + lower))
            turned = scale * jnp.concatenate([-applied[mid:], applied[:mid]], axis=0)
            state[b] = turned
            out_ref[b] = out_ref[b] + turned

        sym_rows().wait_send()
        sym_low().wait_send()
        for b in range(n_local):
            for g in range(2):
                for k in range(half):
                    ag_out(b, g, k).wait_send()
                    rs_copy(b, g, k).wait_send()
        return carry

    lax.fori_loop(0, 2, step, 0)


def local(coefficients, dipole, energies, pulse_field, live_states):
    n_local, n_rows, n_cols = coefficients.shape
    n = lax.axis_size("slab")
    n_sym_dev = lax.axis_size("sym")
    width = dipole.shape[2] // n
    first_block = lax.axis_index("sym") * n_local
    live_here = lax.dynamic_slice_in_dim(live_states, first_block, n_local)
    row_ids = lax.axis_index("slab") * n_rows + jnp.arange(n_rows, dtype=jnp.int32)
    live_mask = (row_ids[None, :] < live_here[:, None]).astype(jnp.float32)[:, None, :]
    column_gain = jnp.concatenate([pulse_field, pulse_field])[:, None]
    start_state = live_mask * jnp.transpose(coefficients, (0, 2, 1))
    half = n // 2
    hops = (2, n_local, 2, half)
    f32, bf16 = jnp.float32, jnp.bfloat16
    vmem = pl.BlockSpec(memory_space=pltpu.VMEM)
    hbm = pl.BlockSpec(memory_space=pl.ANY)
    dma = pltpu.SemaphoreType.DMA
    flops = 8 * n_local * n_rows * dipole.shape[2] * n_cols
    adjoint = pl.pallas_call(
        functools.partial(kernel, n, n_sym_dev),
        out_shape=jax.ShapeDtypeStruct((n_local, n_cols, n_rows), f32),
        in_specs=[hbm, hbm, vmem, vmem, vmem],
        out_specs=vmem,
        scratch_shapes=[
            pltpu.VMEM((n_local, n, n_rows, width), bf16),
            pltpu.VMEM((2, n_local, n, n_rows, n_cols), bf16),
            pltpu.VMEM((n_local, 2, half, n_cols, n_rows), bf16),
            pltpu.VMEM((2, n_local, 2, half, n_cols, n_rows), bf16),
            pltpu.VMEM((n_rows, n_cols), bf16),
            pltpu.VMEM((n_local, n_cols, n_rows), bf16),
            pltpu.VMEM((n_local, n_rows, n_cols), f32),
            pltpu.VMEM((n_local, n_cols, n_rows), f32),
            pltpu.VMEM((max(1, n_local - 1), n_cols, n_rows), f32),
            pltpu.VMEM((n_cols, n_rows), f32),
            pltpu.VMEM((2, n_cols, n_rows), f32),
            dma((n_local, n)),
            dma,
            dma(hops), dma(hops), dma(hops), dma(hops),
            dma((2, 2)), dma((2, 2)),
        ],
        compiler_params=pltpu.CompilerParams(
            collective_id=0, has_side_effects=True, vmem_limit_bytes=62 * 2**20
        ),
        cost_estimate=pl.CostEstimate(flops=flops, bytes_accessed=2 * dipole.size, transcendentals=0),
    )(start_state, dipole, energies[:, None, :], live_mask, column_gain)
    return jnp.transpose(adjoint, (0, 2, 1))


def solution(mesh):
    placed = (P("sym", "slab", None), P("sym", "slab", None), P("sym", "slab"), P(), P())
    return jax.shard_map(
        local, mesh=mesh, in_specs=placed, out_specs=P("sym", "slab", None), check_vma=False
    )
```

```python
import functools

import jax
import jax.numpy as jnp
from jax import lax
from jax.experimental import pallas as pl
from jax.experimental.pallas import tpu as pltpu
from jax.sharding import PartitionSpec as P

step_size = 0.2
MESH = pl.DeviceIdType.MESH


def kernel(
    n, n_sym_dev, start_ref, dip_ref, energy_ref, mask_ref, gain_ref, out_ref,
    dip, gath, rs_send, rs_recv, u_rows, u_cols, acc, state, low, low_send, low_recv,
    load_sem, start_sem, ag_send_sem, ag_recv_sem, rs_send_sem, rs_recv_sem, sym_send_sem, sym_recv_sem,
):
    n_local, cols, rows = out_ref.shape
    width = dip.shape[-1]
    half = n // 2
    side = rows // 2
    mid = cols // 2
    s = lax.axis_index("sym")
    me = lax.axis_index("slab")
    odd = me % 2
    pos = (1 - odd) * (me // 2) + odd * (n - 1 - me // 2)

    def at(offset):
        place = (pos + offset + n) % n
        back = place // half
        return (1 - back) * (2 * place) + back * (2 * (n - place) - 1)

    ring = (at(1), at(-1))
    sym_up = (s + 1) % n_sym_dev
    sym_down = (s + n_sym_dev - 1) % n_sym_dev
    sign = (1, -1)

    barrier = pltpu.get_barrier_semaphore()
    for peer in ((s, ring[0]), (s, ring[1]), (sym_up, me), (sym_down, me)):
        pl.semaphore_signal(barrier, inc=1, device_id=peer, device_id_type=MESH)

    def load(b, d):
        j = at(half + d)
        return pltpu.make_async_copy(
            dip_ref.at[b, :, pl.ds(pl.multiple_of(j * width, width), width)],
            dip.at[b, j],
            load_sem.at[b, d],
        )

    def start_load(b):
        def one(d, carry):
            load(b, d).start()
            return carry

        return one

    def wait_load(b):
        def one(d, carry):
            load(b, d).wait()
            return carry

        return one

    first_state = pltpu.make_async_copy(start_ref, state, start_sem)
    first_state.start()
    lax.fori_loop(0, n, start_load(0), 0)
    lax.fori_loop(0, n, start_load(1), 0)
    first_state.wait()

    def ag_copy(h, b, g, k, owner):
        slot = gath.at[h, b, owner]
        if k == half - 1:
            slot = gath.at[h, b, owner, pl.ds(g * side, side)]
        return pltpu.make_async_remote_copy(
            src_ref=slot, dst_ref=slot,
            send_sem=ag_send_sem.at[h, b, g, k], recv_sem=ag_recv_sem.at[h, b, g, k],
            device_id=(s, ring[g]), device_id_type=MESH,
        )

    def ag_out(h, b, g, k):
        return ag_copy(h, b, g, k, at(-sign[g] * k))

    def ag_in(h, b, g, k):
        return ag_copy(h, b, g, k, at(-sign[g] * (k + 1)))

    def rs_copy(h, b, g, k):
        source, target = rs_send.at[b, g, k], rs_recv.at[h, b, g, k]
        if k == 0:
            piece = pl.ds(g * mid, mid)
            source, target = rs_send.at[b, g, k, piece], rs_recv.at[h, b, g, k, piece]
        return pltpu.make_async_remote_copy(
            src_ref=source, dst_ref=target,
            send_sem=rs_send_sem.at[h, b, g, k], recv_sem=rs_recv_sem.at[h, b, g, k],
            device_id=(s, ring[g]), device_id_type=MESH,
        )

    def sym_rows(h):
        return pltpu.make_async_remote_copy(
            src_ref=u_rows, dst_ref=gath.at[h, 1, me],
            send_sem=sym_send_sem.at[h, 0], recv_sem=sym_recv_sem.at[h, 0],
            device_id=(sym_down, me), device_id_type=MESH,
        )

    def sym_low(h):
        return pltpu.make_async_remote_copy(
            src_ref=low_send, dst_ref=low_recv.at[h],
            send_sem=sym_send_sem.at[h, 1], recv_sem=sym_recv_sem.at[h, 1],
            device_id=(sym_up, me), device_id_type=MESH,
        )

    tile = min(256, width)
    row_tile = min(256, rows)

    def over_tiles(h, b, j, emit):
        def one(t, c):
            piece = pl.ds(pl.multiple_of(t * tile, tile), tile)
            emit(piece, jnp.dot(u_cols[h, b], dip[b, j, :, piece], preferred_element_type=jnp.float32))
            return c

        lax.fori_loop(0, width // tile, one, 0)

    def add_hop(h, b, g, k, piece, value):
        if k == 0:
            got = rs_recv[h, b, g, 0, g * mid:(g + 1) * mid, piece].astype(jnp.float32)
            parts = [value[:mid], value[mid:]]
            parts[g] = parts[g] + got
            return jnp.concatenate(parts, axis=0)
        return value + rs_recv[h, b, g, k, :, piece].astype(jnp.float32)

    def rs_free(h, b, g, k):
        if h == 1:
            rs_copy(0, b, g, k).wait_send()

    def rs_first(h, b):
        def emit(piece, value):
            value = value.astype(jnp.bfloat16)
            rs_send[b, 0, 0, :mid, piece] = value[:mid]
            rs_send[b, 1, 0, mid:, piece] = value[mid:]

        for g in range(2):
            rs_free(h, b, g, 0)
        over_tiles(h, b, at(half), emit)
        for g in range(2):
            rs_copy(h, b, g, 0).start()

    def rs_hop(h, b, g, k):
        rs_free(h, b, g, k)
        rs_copy(h, b, g, k - 1).wait_recv()

        def emit(piece, value):
            rs_send[b, g, k, :, piece] = add_hop(h, b, g, k - 1, piece, value).astype(jnp.bfloat16)

        over_tiles(h, b, at(sign[g] * (half - k)), emit)
        rs_copy(h, b, g, k).start()

    def rs_last(h, b, target):
        for g in range(2):
            rs_copy(h, b, g, half - 1).wait_recv()

        def emit(piece, value):
            for g in range(2):
                value = add_hop(h, b, g, half - 1, piece, value)
            target[:, piece] = value

        over_tiles(h, b, me, emit)

    def forward(h, b, j, first=False):
        def one(t, c):
            piece = pl.ds(pl.multiple_of(t * row_tile, row_tile), row_tile)
            value = jnp.dot(dip[b, j, piece, :], gath[h, b, j], preferred_element_type=jnp.float32)
            acc[h, b, piece, :] = value if first else acc[h, b, piece, :] + value
            return c

        lax.fori_loop(0, rows // row_tile, one, 0)

    def present(h, b):
        if b == 0:
            if h == 1:
                sym_rows(0).wait_send()
            u_rows[...] = state[0].T.astype(jnp.bfloat16)
            sym_rows(h).start()
        else:
            gath[h, 0, me] = state[1].T.astype(jnp.bfloat16)
        u_cols[h, b] = state[b].astype(jnp.bfloat16)

    def begin(h, c):
        if c == 0:
            for g in range(2):
                ag_out(h, 0, g, 0).start()
        rs_first(h, 1 - c)
        if c == 1:
            sym_rows(h).wait_recv()
            for g in range(2):
                ag_out(h, 1, g, 0).start()

    def finish(h, c):
        upper = acc[h, c].T
        if c == 0:
            sym_low(h).wait_recv()
            lower = low_recv[h] * (s > 0).astype(jnp.float32)
        else:
            lower = low[...]
            upper = upper * (s < n_sym_dev - 1).astype(jnp.float32)
        applied = mask_ref[c] * (energy_ref[c] * state[c] + gain_ref[...] * (upper + lower))
        turned = step_size / (h + 1) * jnp.concatenate([-applied[mid:], applied[:mid]], axis=0)
        if h == 0:
            out_ref[c] = state[c] + turned
            state[c] = turned
            present(1, c)
        else:
            out_ref[c] = out_ref[c] + turned

    lag = 1
    begins = {(0, 1): 0, (0, 0): lag, (1, 0): half, (1, 1): half + lag}
    present(0, 1)
    pl.semaphore_wait(barrier, 4)
    present(0, 0)
    for t in range(2 * half + lag + 1):
        live = [(h, c, t - begins[h, c]) for h, c in begins if 0 <= t - begins[h, c] <= half]
        for h, c, k in live:
            if k > 0:
                for g in range(2):
                    ag_in(h, c, g, k - 1).wait_recv()
                    if k < half:
                        ag_out(h, c, g, k).start()
        if t == 1:
            lax.fori_loop(1, n, wait_load(0), 0)
        for h, c, k in live:
            if 0 < k < half:
                for g in range(2):
                    rs_hop(h, 1 - c, g, k)
            if k == half:
                if c == 0:
                    if h == 1:
                        sym_low(0).wait_send()
                    rs_last(h, 1, low_send)
                    sym_low(h).start()
                else:
                    rs_last(h, 0, low)
        if t == 1:
            lax.fori_loop(0, n, wait_load(1), 0)
        for h, c, k in live:
            if k == 1:
                forward(h, c, me, first=True)
            if 0 < k < half:
                for g in range(2):
                    forward(h, c, at(-sign[g] * k))
            if k == half:
                forward(h, c, at(half))
                finish(h, c)
        for h, c, k in live:
            if k == 0:
                if t == 0:
                    load(0, 0).wait()
                begin(h, c)

    sym_rows(1).wait_send()
    sym_low(1).wait_send()
    for b in range(2):
        for g in range(2):
            for k in range(half):
                rs_copy(1, b, g, k).wait_send()
                for h in range(2):
                    ag_out(h, b, g, k).wait_send()


def local(coefficients, dipole, energies, pulse_field, live_states):
    n_local, n_rows, n_cols = coefficients.shape
    assert n_local == 2
    n = lax.axis_size("slab")
    n_sym_dev = lax.axis_size("sym")
    width = dipole.shape[2] // n
    first_block = lax.axis_index("sym") * n_local
    live_here = lax.dynamic_slice_in_dim(live_states, first_block, n_local)
    row_ids = lax.axis_index("slab") * n_rows + jnp.arange(n_rows, dtype=jnp.int32)
    live_mask = (row_ids[None, :] < live_here[:, None]).astype(jnp.float32)[:, None, :]
    column_gain = jnp.concatenate([pulse_field, pulse_field])[:, None]
    start_state = live_mask * jnp.transpose(coefficients, (0, 2, 1))
    half = n // 2
    hops = (2, n_local, 2, half)
    f32, bf16 = jnp.float32, jnp.bfloat16
    vmem = pl.BlockSpec(memory_space=pltpu.VMEM)
    hbm = pl.BlockSpec(memory_space=pl.ANY)
    dma = pltpu.SemaphoreType.DMA
    flops = 8 * n_local * n_rows * dipole.shape[2] * n_cols
    adjoint = pl.pallas_call(
        functools.partial(kernel, n, n_sym_dev),
        out_shape=jax.ShapeDtypeStruct((n_local, n_cols, n_rows), f32),
        in_specs=[hbm, hbm, vmem, vmem, vmem],
        out_specs=vmem,
        scratch_shapes=[
            pltpu.VMEM((n_local, n, n_rows, width), bf16),
            pltpu.VMEM((2, n_local, n, n_rows, n_cols), bf16),
            pltpu.VMEM((n_local, 2, half, n_cols, n_rows), bf16),
            pltpu.VMEM((2, n_local, 2, half, n_cols, n_rows), bf16),
            pltpu.VMEM((n_rows, n_cols), bf16),
            pltpu.VMEM((2, n_local, n_cols, n_rows), bf16),
            pltpu.VMEM((2, n_local, n_rows, n_cols), f32),
            pltpu.VMEM((n_local, n_cols, n_rows), f32),
            pltpu.VMEM((n_cols, n_rows), f32),
            pltpu.VMEM((n_cols, n_rows), f32),
            pltpu.VMEM((2, n_cols, n_rows), f32),
            dma((n_local, n)),
            dma,
            dma(hops), dma(hops), dma(hops), dma(hops),
            dma((2, 2)), dma((2, 2)),
        ],
        compiler_params=pltpu.CompilerParams(
            collective_id=0, has_side_effects=True, vmem_limit_bytes=62 * 2**20
        ),
        cost_estimate=pl.CostEstimate(flops=flops, bytes_accessed=2 * dipole.size, transcendentals=0),
    )(start_state, dipole, energies[:, None, :], live_mask, column_gain)
    return jnp.transpose(adjoint, (0, 2, 1))


def solution(mesh):
    placed = (P("sym", "slab", None), P("sym", "slab", None), P("sym", "slab"), P(), P())
    return jax.shard_map(
        local, mesh=mesh, in_specs=placed, out_specs=P("sym", "slab", None), check_vma=False
    )
```

```python
import functools

import jax
import jax.numpy as jnp
from jax import lax
from jax.experimental import pallas as pl
from jax.experimental.pallas import tpu as pltpu
from jax.sharding import PartitionSpec as P

step_size = 0.2
MESH = pl.DeviceIdType.MESH


def kernel(
    n, n_sym_dev, coef_ref, dip_ref, energy_ref, field_ref, live_ref, out_ref,
    dip, gath, rs_send, rs_recv, u_rows, u_cols, acc, state, low, low_send, low_recv,
    load_sem, start_sem, ag_send_sem, ag_recv_sem, rs_send_sem, rs_recv_sem, sym_send_sem, sym_recv_sem,
):
    n_local, cols, rows = out_ref.shape
    width = dip.shape[-1]
    half = n // 2
    side = rows // 2
    mid = cols // 2
    s = lax.axis_index("sym")
    me = lax.axis_index("slab")
    odd = me % 2
    pos = (1 - odd) * (me // 2) + odd * (n - 1 - me // 2)

    def at(offset):
        place = (pos + offset + n) % n
        back = place // half
        return (1 - back) * (2 * place) + back * (2 * (n - place) - 1)

    ring = (at(1), at(-1))
    sym_up = (s + 1) % n_sym_dev
    sym_down = (s + n_sym_dev - 1) % n_sym_dev
    sign = (1, -1)

    barrier = pltpu.get_barrier_semaphore()
    for peer in ((s, ring[0]), (s, ring[1]), (sym_up, me), (sym_down, me)):
        pl.semaphore_signal(barrier, inc=1, device_id=peer, device_id_type=MESH)

    def load(b, d):
        j = at(half + d)
        return pltpu.make_async_copy(
            dip_ref.at[b, :, pl.ds(pl.multiple_of(j * width, width), width)],
            dip.at[b, j],
            load_sem.at[b, d],
        )

    def start_load(b):
        def one(d, carry):
            load(b, d).start()
            return carry

        return one

    def wait_load(b):
        def one(d, carry):
            load(b, d).wait()
            return carry

        return one

    first_state = pltpu.make_async_copy(coef_ref, acc.at[1], start_sem)
    first_state.start()
    lax.fori_loop(0, n, start_load(0), 0)
    lax.fori_loop(0, n, start_load(1), 0)
    gain = jnp.concatenate([field_ref[...], field_ref[...]], axis=1)
    gain = jnp.broadcast_to(gain, (cols, cols)).T[:, :1]
    row_ids = me * rows + lax.broadcasted_iota(jnp.int32, (1, rows), 1)
    mask = [(row_ids < live_ref[s * 2 + b]).astype(jnp.float32) for b in range(2)]
    first_state.wait()
    for b in range(2):
        state[b] = mask[b] * acc[1, b].T

    def ag_copy(h, b, g, k, owner):
        slot = gath.at[h, b, owner]
        if k == half - 1:
            slot = gath.at[h, b, owner, pl.ds(g * side, side)]
        return pltpu.make_async_remote_copy(
            src_ref=slot, dst_ref=slot,
            send_sem=ag_send_sem.at[h, b, g, k], recv_sem=ag_recv_sem.at[h, b, g, k],
            device_id=(s, ring[g]), device_id_type=MESH,
        )

    def ag_out(h, b, g, k):
        return ag_copy(h, b, g, k, at(-sign[g] * k))

    def ag_in(h, b, g, k):
        return ag_copy(h, b, g, k, at(-sign[g] * (k + 1)))

    def rs_copy(h, b, g, k):
        source, target = rs_send.at[b, g, k], rs_recv.at[h, b, g, k]
        if k == 0:
            piece = pl.ds(g * mid, mid)
            source, target = rs_send.at[b, g, k, piece], rs_recv.at[h, b, g, k, piece]
        return pltpu.make_async_remote_copy(
            src_ref=source, dst_ref=target,
            send_sem=rs_send_sem.at[h, b, g, k], recv_sem=rs_recv_sem.at[h, b, g, k],
            device_id=(s, ring[g]), device_id_type=MESH,
        )

    def sym_rows(h):
        return pltpu.make_async_remote_copy(
            src_ref=u_rows, dst_ref=gath.at[h, 1, me],
            send_sem=sym_send_sem.at[h, 0], recv_sem=sym_recv_sem.at[h, 0],
            device_id=(sym_down, me), device_id_type=MESH,
        )

    def sym_low(h):
        return pltpu.make_async_remote_copy(
            src_ref=low_send, dst_ref=low_recv.at[h],
            send_sem=sym_send_sem.at[h, 1], recv_sem=sym_recv_sem.at[h, 1],
            device_id=(sym_up, me), device_id_type=MESH,
        )

    tile = min(256, width)
    row_tile = min(256, rows)

    def over_tiles(h, b, j, emit):
        def one(t, c):
            piece = pl.ds(pl.multiple_of(t * tile, tile), tile)
            emit(piece, jnp.dot(u_cols[h, b], dip[b, j, :, piece], preferred_element_type=jnp.float32))
            return c

        lax.fori_loop(0, width // tile, one, 0)

    def add_hop(h, b, g, k, piece, value):
        if k == 0:
            got = rs_recv[h, b, g, 0, g * mid:(g + 1) * mid, piece].astype(jnp.float32)
            parts = [value[:mid], value[mid:]]
            parts[g] = parts[g] + got
            return jnp.concatenate(parts, axis=0)
        return value + rs_recv[h, b, g, k, :, piece].astype(jnp.float32)

    def rs_free(h, b, g, k):
        if h == 1:
            rs_copy(0, b, g, k).wait_send()

    def rs_first(h, b):
        def emit(piece, value):
            value = value.astype(jnp.bfloat16)
            rs_send[b, 0, 0, :mid, piece] = value[:mid]
            rs_send[b, 1, 0, mid:, piece] = value[mid:]

        for g in range(2):
            rs_free(h, b, g, 0)
        over_tiles(h, b, at(half), emit)
        for g in range(2):
            rs_copy(h, b, g, 0).start()

    def rs_hop(h, b, g, k):
        rs_free(h, b, g, k)
        rs_copy(h, b, g, k - 1).wait_recv()

        def emit(piece, value):
            rs_send[b, g, k, :, piece] = add_hop(h, b, g, k - 1, piece, value).astype(jnp.bfloat16)

        over_tiles(h, b, at(sign[g] * (half - k)), emit)
        rs_copy(h, b, g, k).start()

    def rs_last(h, b, target):
        for g in range(2):
            rs_copy(h, b, g, half - 1).wait_recv()

        def emit(piece, value):
            for g in range(2):
                value = add_hop(h, b, g, half - 1, piece, value)
            target[:, piece] = value

        over_tiles(h, b, me, emit)

    def forward(h, b, j, first=False):
        def one(t, c):
            piece = pl.ds(pl.multiple_of(t * row_tile, row_tile), row_tile)
            value = jnp.dot(dip[b, j, piece, :], gath[h, b, j], preferred_element_type=jnp.float32)
            acc[h, b, piece, :] = value if first else acc[h, b, piece, :] + value
            return c

        lax.fori_loop(0, rows // row_tile, one, 0)

    def present(h, b):
        if b == 0:
            if h == 1:
                sym_rows(0).wait_send()
            u_rows[...] = state[0].T.astype(jnp.bfloat16)
            sym_rows(h).start()
        else:
            gath[h, 0, me] = state[1].T.astype(jnp.bfloat16)
        u_cols[h, b] = state[b].astype(jnp.bfloat16)

    def begin(h, c):
        if c == 0:
            for g in range(2):
                ag_out(h, 0, g, 0).start()
        rs_first(h, 1 - c)
        if c == 1:
            sym_rows(h).wait_recv()
            for g in range(2):
                ag_out(h, 1, g, 0).start()

    def finish(h, c):
        upper = acc[h, c].T
        if c == 0:
            sym_low(h).wait_recv()
            lower = low_recv[h] * (s > 0).astype(jnp.float32)
        else:
            lower = low[...]
            upper = upper * (s < n_sym_dev - 1).astype(jnp.float32)
        applied = mask[c] * (energy_ref[c:c + 1] * state[c] + gain * (upper + lower))
        turned = step_size / (h + 1) * jnp.concatenate([-applied[mid:], applied[:mid]], axis=0)
        if h == 0:
            out_ref[c] = state[c] + turned
            state[c] = turned
            present(1, c)
        else:
            out_ref[c] = out_ref[c] + turned

    lag = 1
    begins = {(0, 1): 0, (0, 0): lag, (1, 0): half, (1, 1): half + lag}
    present(0, 1)
    pl.semaphore_wait(barrier, 4)
    present(0, 0)
    for t in range(2 * half + lag + 1):
        live = [(h, c, t - begins[h, c]) for h, c in begins if 0 <= t - begins[h, c] <= half]
        for h, c, k in live:
            if k > 0:
                for g in range(2):
                    ag_in(h, c, g, k - 1).wait_recv()
                    if k < half:
                        ag_out(h, c, g, k).start()
        if t == 1:
            lax.fori_loop(1, n, wait_load(0), 0)
        for h, c, k in live:
            if 0 < k < half:
                for g in range(2):
                    rs_hop(h, 1 - c, g, k)
            if k == half:
                if c == 0:
                    if h == 1:
                        sym_low(0).wait_send()
                    rs_last(h, 1, low_send)
                    sym_low(h).start()
                else:
                    rs_last(h, 0, low)
        if t == 1:
            lax.fori_loop(0, n, wait_load(1), 0)
        for h, c, k in live:
            if k == 1:
                forward(h, c, me, first=True)
            if 0 < k < half:
                for g in range(2):
                    forward(h, c, at(-sign[g] * k))
            if k == half:
                forward(h, c, at(half))
                finish(h, c)
        for h, c, k in live:
            if k == 0:
                if t == 0:
                    load(0, 0).wait()
                begin(h, c)

    sym_rows(1).wait_send()
    sym_low(1).wait_send()
    for b in range(2):
        for g in range(2):
            for k in range(half):
                rs_copy(1, b, g, k).wait_send()
                for h in range(2):
                    ag_out(h, b, g, k).wait_send()


def local(coefficients, dipole, energies, pulse_field, live_states):
    n_local, n_rows, n_cols = coefficients.shape
    assert n_local == 2
    n = lax.axis_size("slab")
    n_sym_dev = lax.axis_size("sym")
    width = dipole.shape[2] // n
    half = n // 2
    hops = (2, n_local, 2, half)
    f32, bf16 = jnp.float32, jnp.bfloat16
    vmem = pl.BlockSpec(memory_space=pltpu.VMEM)
    hbm = pl.BlockSpec(memory_space=pl.ANY)
    dma = pltpu.SemaphoreType.DMA
    flops = 8 * n_local * n_rows * dipole.shape[2] * n_cols
    adjoint = pl.pallas_call(
        functools.partial(kernel, n, n_sym_dev),
        out_shape=jax.ShapeDtypeStruct((n_local, n_cols, n_rows), f32),
        in_specs=[hbm, hbm, vmem, vmem, pl.BlockSpec(memory_space=pltpu.SMEM)],
        out_specs=vmem,
        scratch_shapes=[
            pltpu.VMEM((n_local, n, n_rows, width), bf16),
            pltpu.VMEM((2, n_local, n, n_rows, n_cols), bf16),
            pltpu.VMEM((n_local, 2, half, n_cols, n_rows), bf16),
            pltpu.VMEM((2, n_local, 2, half, n_cols, n_rows), bf16),
            pltpu.VMEM((n_rows, n_cols), bf16),
            pltpu.VMEM((2, n_local, n_cols, n_rows), bf16),
            pltpu.VMEM((2, n_local, n_rows, n_cols), f32),
            pltpu.VMEM((n_local, n_cols, n_rows), f32),
            pltpu.VMEM((n_cols, n_rows), f32),
            pltpu.VMEM((n_cols, n_rows), f32),
            pltpu.VMEM((2, n_cols, n_rows), f32),
            dma((n_local, n)),
            dma,
            dma(hops), dma(hops), dma(hops), dma(hops),
            dma((2, 2)), dma((2, 2)),
        ],
        compiler_params=pltpu.CompilerParams(
            collective_id=0, has_side_effects=True, vmem_limit_bytes=62 * 2**20
        ),
        cost_estimate=pl.CostEstimate(flops=flops, bytes_accessed=2 * dipole.size, transcendentals=0),
    )(coefficients, dipole, energies, pulse_field[None, :], live_states)
    return jnp.transpose(adjoint, (0, 2, 1))


def solution(mesh):
    placed = (P("sym", "slab", None), P("sym", "slab", None), P("sym", "slab"), P(), P())
    return jax.shard_map(
        local, mesh=mesh, in_specs=placed, out_specs=P("sym", "slab", None), check_vma=False
    )
```

```python
import functools

import jax
import jax.numpy as jnp
from jax import lax
from jax.experimental import pallas as pl
from jax.experimental.pallas import tpu as pltpu
from jax.sharding import PartitionSpec as P

step_size = 0.2
MESH = pl.DeviceIdType.MESH


def kernel(
    n, n_sym_dev, coef_ref, dip_ref, energy_ref, field_ref, live_ref, out_ref,
    dip, gath, rs_send, rs_recv, u_rows, u_cols, acc, state, low, low_send, low_recv,
    load_sem, start_sem, ag_send_sem, ag_recv_sem, rs_send_sem, rs_recv_sem, sym_send_sem, sym_recv_sem,
):
    n_local, cols, rows = out_ref.shape
    width = dip.shape[-1]
    half = n // 2
    side = rows // 2
    mid = cols // 2
    s = lax.axis_index("sym")
    me = lax.axis_index("slab")
    odd = me % 2
    pos = (1 - odd) * (me // 2) + odd * (n - 1 - me // 2)

    def at(offset):
        place = (pos + offset + n) % n
        back = place // half
        return (1 - back) * (2 * place) + back * (2 * (n - place) - 1)

    ring = (at(1), at(-1))
    sym_up = (s + 1) % n_sym_dev
    sym_down = (s + n_sym_dev - 1) % n_sym_dev
    sign = (1, -1)

    barrier = pltpu.get_barrier_semaphore()
    for peer in ((s, ring[0]), (s, ring[1]), (sym_up, me), (sym_down, me)):
        pl.semaphore_signal(barrier, inc=1, device_id=peer, device_id_type=MESH)

    def load(b, d):
        j = at(half + d)
        return pltpu.make_async_copy(
            dip_ref.at[b, :, pl.ds(pl.multiple_of(j * width, width), width)],
            dip.at[b, j],
            load_sem.at[b, d],
        )

    def start_load(b):
        def one(d, carry):
            load(b, d).start()
            return carry

        return one

    def wait_load(b):
        def one(d, carry):
            load(b, d).wait()
            return carry

        return one

    first_state = pltpu.make_async_copy(coef_ref, acc.at[1], start_sem)
    first_state.start()
    lax.fori_loop(0, n, start_load(0), 0)
    lax.fori_loop(0, n, start_load(1), 0)
    gain = jnp.concatenate([field_ref[...], field_ref[...]], axis=1)
    gain = jnp.broadcast_to(gain, (cols, cols)).T[:, :1]
    row_ids = me * rows + lax.broadcasted_iota(jnp.int32, (1, rows), 1)
    mask = [(row_ids < live_ref[s * 2 + b]).astype(jnp.float32) for b in range(2)]
    first_state.wait()
    for b in range(2):
        state[b] = mask[b] * acc[1, b].T

    def ag_copy(h, b, g, k, owner):
        slot = gath.at[h, b, owner]
        if k == half - 1:
            slot = gath.at[h, b, owner, pl.ds(g * side, side)]
        return pltpu.make_async_remote_copy(
            src_ref=slot, dst_ref=slot,
            send_sem=ag_send_sem.at[h, b, g, k], recv_sem=ag_recv_sem.at[h, b, g, k],
            device_id=(s, ring[g]), device_id_type=MESH,
        )

    def ag_out(h, b, g, k):
        return ag_copy(h, b, g, k, at(-sign[g] * k))

    def ag_in(h, b, g, k):
        return ag_copy(h, b, g, k, at(-sign[g] * (k + 1)))

    def rs_copy(h, b, g, k):
        source, target = rs_send.at[b, g, k], rs_recv.at[h, b, g, k]
        if k == 0:
            piece = pl.ds(g * mid, mid)
            source, target = rs_send.at[b, g, k, piece], rs_recv.at[h, b, g, k, piece]
        return pltpu.make_async_remote_copy(
            src_ref=source, dst_ref=target,
            send_sem=rs_send_sem.at[h, b, g, k], recv_sem=rs_recv_sem.at[h, b, g, k],
            device_id=(s, ring[g]), device_id_type=MESH,
        )

    def sym_rows(h):
        return pltpu.make_async_remote_copy(
            src_ref=u_rows, dst_ref=gath.at[h, 1, me],
            send_sem=sym_send_sem.at[h, 0], recv_sem=sym_recv_sem.at[h, 0],
            device_id=(sym_down, me), device_id_type=MESH,
        )

    def sym_low(h):
        return pltpu.make_async_remote_copy(
            src_ref=low_send, dst_ref=low_recv.at[h],
            send_sem=sym_send_sem.at[h, 1], recv_sem=sym_recv_sem.at[h, 1],
            device_id=(sym_up, me), device_id_type=MESH,
        )

    tile = min(256, width)
    row_tile = min(256, rows)

    def over_tiles(h, b, j, emit):
        def one(t, c):
            piece = pl.ds(pl.multiple_of(t * tile, tile), tile)
            emit(piece, jnp.dot(u_cols[h, b], dip[b, j, :, piece], preferred_element_type=jnp.float32))
            return c

        lax.fori_loop(0, width // tile, one, 0)

    def add_hop(h, b, g, k, piece, value):
        if k == 0:
            got = rs_recv[h, b, g, 0, g * mid:(g + 1) * mid, piece].astype(jnp.float32)
            parts = [value[:mid], value[mid:]]
            parts[g] = parts[g] + got
            return jnp.concatenate(parts, axis=0)
        return value + rs_recv[h, b, g, k, :, piece].astype(jnp.float32)

    def rs_free(h, b, g, k):
        if h == 1:
            rs_copy(0, b, g, k).wait_send()

    def rs_first(h, b):
        def emit(piece, value):
            value = value.astype(jnp.bfloat16)
            rs_send[b, 0, 0, :mid, piece] = value[:mid]
            rs_send[b, 1, 0, mid:, piece] = value[mid:]

        for g in range(2):
            rs_free(h, b, g, 0)
        over_tiles(h, b, at(half), emit)
        for g in range(2):
            rs_copy(h, b, g, 0).start()

    def rs_hop(h, b, g, k):
        rs_free(h, b, g, k)
        rs_copy(h, b, g, k - 1).wait_recv()

        def emit(piece, value):
            rs_send[b, g, k, :, piece] = add_hop(h, b, g, k - 1, piece, value).astype(jnp.bfloat16)

        over_tiles(h, b, at(sign[g] * (half - k)), emit)
        rs_copy(h, b, g, k).start()

    def rs_last(h, b, target):
        for g in range(2):
            rs_copy(h, b, g, half - 1).wait_recv()

        def emit(piece, value):
            for g in range(2):
                value = add_hop(h, b, g, half - 1, piece, value)
            target[:, piece] = value

        over_tiles(h, b, me, emit)

    def forward(h, b, j, first=False):
        def one(t, c):
            piece = pl.ds(pl.multiple_of(t * row_tile, row_tile), row_tile)
            value = jnp.dot(dip[b, j, piece, :], gath[h, b, j], preferred_element_type=jnp.float32)
            acc[h, b, piece, :] = value if first else acc[h, b, piece, :] + value
            return c

        lax.fori_loop(0, rows // row_tile, one, 0)

    def present(h, b):
        if b == 0:
            if h == 1:
                sym_rows(0).wait_send()
            u_rows[...] = state[0].T.astype(jnp.bfloat16)
            sym_rows(h).start()
        else:
            gath[h, 0, me] = state[1].T.astype(jnp.bfloat16)
        u_cols[h, b] = state[b].astype(jnp.bfloat16)

    def begin(h, c):
        if c == 0 and h == 1:
            for g in range(2):
                ag_out(h, 0, g, 0).start()
        rs_first(h, 1 - c)
        if c == 1:
            sym_rows(h).wait_recv()
            for g in range(2):
                ag_out(h, 1, g, 0).start()

    def finish(h, c):
        upper = acc[h, c].T
        if c == 0:
            sym_low(h).wait_recv()
            lower = low_recv[h] * (s > 0).astype(jnp.float32)
        else:
            lower = low[...]
            upper = upper * (s < n_sym_dev - 1).astype(jnp.float32)
        applied = mask[c] * (energy_ref[c:c + 1] * state[c] + gain * (upper + lower))
        turned = step_size / (h + 1) * jnp.concatenate([-applied[mid:], applied[:mid]], axis=0)
        if h == 0:
            out_ref[c] = state[c] + turned
            state[c] = turned
            present(1, c)
        else:
            out_ref[c] = out_ref[c] + turned

    lag = 2
    begins = {(0, 1): 0, (0, 0): lag, (1, 0): half, (1, 1): half + lag}
    present(0, 1)
    pl.semaphore_wait(barrier, 4)
    for g in range(2):
        ag_out(0, 0, g, 0).start()
    present(0, 0)
    for t in range(2 * half + lag + 1):
        live = [(h, c, t - begins[h, c]) for h, c in begins if 0 <= t - begins[h, c] <= half]
        for h, c, k in live:
            if k > 0:
                for g in range(2):
                    ag_in(h, c, g, k - 1).wait_recv()
                    if k < half:
                        ag_out(h, c, g, k).start()
        if t == 1:
            lax.fori_loop(1, n, wait_load(0), 0)
        for h, c, k in live:
            if 0 < k < half:
                for g in range(2):
                    rs_hop(h, 1 - c, g, k)
            if k == half:
                if c == 0:
                    if h == 1:
                        sym_low(0).wait_send()
                    rs_last(h, 1, low_send)
                    sym_low(h).start()
                else:
                    rs_last(h, 0, low)
        if t == 1:
            lax.fori_loop(0, n, wait_load(1), 0)
        for h, c, k in live:
            if k == 1:
                forward(h, c, me, first=True)
            if 0 < k < half:
                for g in range(2):
                    forward(h, c, at(-sign[g] * k))
            if k == half:
                forward(h, c, at(half))
                finish(h, c)
        for h, c, k in live:
            if k == 0:
                if t == 0:
                    load(0, 0).wait()
                begin(h, c)

    sym_rows(1).wait_send()
    sym_low(1).wait_send()
    for b in range(2):
        for g in range(2):
            for k in range(half):
                rs_copy(1, b, g, k).wait_send()
                for h in range(2):
                    ag_out(h, b, g, k).wait_send()


def local(coefficients, dipole, energies, pulse_field, live_states):
    n_local, n_rows, n_cols = coefficients.shape
    assert n_local == 2
    n = lax.axis_size("slab")
    n_sym_dev = lax.axis_size("sym")
    width = dipole.shape[2] // n
    half = n // 2
    hops = (2, n_local, 2, half)
    f32, bf16 = jnp.float32, jnp.bfloat16
    vmem = pl.BlockSpec(memory_space=pltpu.VMEM)
    hbm = pl.BlockSpec(memory_space=pl.ANY)
    dma = pltpu.SemaphoreType.DMA
    flops = 8 * n_local * n_rows * dipole.shape[2] * n_cols
    adjoint = pl.pallas_call(
        functools.partial(kernel, n, n_sym_dev),
        out_shape=jax.ShapeDtypeStruct((n_local, n_cols, n_rows), f32),
        in_specs=[hbm, hbm, vmem, vmem, pl.BlockSpec(memory_space=pltpu.SMEM)],
        out_specs=vmem,
        scratch_shapes=[
            pltpu.VMEM((n_local, n, n_rows, width), bf16),
            pltpu.VMEM((2, n_local, n, n_rows, n_cols), bf16),
            pltpu.VMEM((n_local, 2, half, n_cols, n_rows), bf16),
            pltpu.VMEM((2, n_local, 2, half, n_cols, n_rows), bf16),
            pltpu.VMEM((n_rows, n_cols), bf16),
            pltpu.VMEM((2, n_local, n_cols, n_rows), bf16),
            pltpu.VMEM((2, n_local, n_rows, n_cols), f32),
            pltpu.VMEM((n_local, n_cols, n_rows), f32),
            pltpu.VMEM((n_cols, n_rows), f32),
            pltpu.VMEM((n_cols, n_rows), f32),
            pltpu.VMEM((2, n_cols, n_rows), f32),
            dma((n_local, n)),
            dma,
            dma(hops), dma(hops), dma(hops), dma(hops),
            dma((2, 2)), dma((2, 2)),
        ],
        compiler_params=pltpu.CompilerParams(
            collective_id=0, has_side_effects=True, vmem_limit_bytes=62 * 2**20
        ),
        cost_estimate=pl.CostEstimate(flops=flops, bytes_accessed=2 * dipole.size, transcendentals=0),
    )(coefficients, dipole, energies, pulse_field[None, :], live_states)
    return jnp.transpose(adjoint, (0, 2, 1))


def solution(mesh):
    placed = (P("sym", "slab", None), P("sym", "slab", None), P("sym", "slab"), P(), P())
    return jax.shard_map(
        local, mesh=mesh, in_specs=placed, out_specs=P("sym", "slab", None), check_vma=False
    )
```
